128 devices in a mesh: seq: 128 (over x, z, y, core).
Axes of the slice: x: 4, y: 4, z: 4, core: 2. Of those that a mesh axis runs over, the one named last changes fastest.
Arguments:
- queries: bfloat16 [131072, 4096], P('seq'), may hold values from -6 to 6
- span_keys: bfloat16 [131072, 1024], P('seq'), may hold values from -6 to 6
- span_values: bfloat16 [131072, 1024], P('seq'), may hold values from -6 to 6
- past_keys: bfloat16 [2, 128, 512, 1024], P(None, 'seq'), may hold values from -6 to 6
- past_values: bfloat16 [2, 128, 512, 1024], P(None, 'seq'), may hold values from -6 to 6
- selected: int32 [256, 8, 4], P('seq'), may hold values from 0 to 255, as said below
Outputs:
- attended: bfloat16 [131072, 4096], P('seq')
The draws below stay inside these ranges and needn't reach their ends.
Inputs may be any that keep to these rules, and one draw needn't show every extreme that they name: `selected`: query blocks k * 2 to (k + 1) * 2 - 1 form group k. Among the 64 numbers of one group, at most 1 are equal modulo 128, and some residue is named exactly 1 times.
All inputs are finite; a program needn't handle non-finite values.
Results may differ from the reference program's by a relative error of at most 0.005.
Values may be sent and summed in bfloat16 or wider, within the bound.
No kernel may reach another device: no remote copies, remote signals or barrier semaphores. Data moves between devices by JAX's collectives and lax.ppermute only.
A program may use at most 256 MiB of HBM per device.

```python
import jax
import jax.numpy as jnp
from jax import lax

QH = 32
KVH = 8
HD = 128
BLOCK = 512
TOPK = 4
QB_DEV = 2
PB_DEV = 2
QTOK = 131072
N_SEQ = 128


def draw_queries(key, part):
    rows = BLOCK * QB_DEV * N_SEQ
    base = jnp.clip(jax.random.normal(jax.random.fold_in(key, 1), (rows, QH * HD), jnp.float32), -6.0, 6.0)
    return base.astype(jnp.bfloat16)


def draw_past_keys(key, part):
    base = jnp.clip(jax.random.normal(jax.random.fold_in(key, 5), (PB_DEV, N_SEQ, BLOCK, KVH * HD), jnp.float32), -6.0, 6.0)
    return base.astype(jnp.bfloat16)


def draw_selected(key, part):
    needed = QB_DEV * KVH * TOPK
    copies = (needed + N_SEQ - 1) // N_SEQ
    pool = jnp.tile(jnp.arange(N_SEQ, dtype=jnp.int32), copies)
    order_keys = jax.random.split(jax.random.fold_in(key, 11), N_SEQ)
    orders = jax.vmap(lambda item: jax.random.permutation(item, pool))(order_keys)
    owners = orders[:, :needed].reshape(N_SEQ * QB_DEV, KVH, TOPK).astype(jnp.int32)
    popular = jax.random.randint(jax.random.fold_in(key, 12), (N_SEQ,), 0, PB_DEV)
    favour = jax.random.randint(jax.random.fold_in(key, 13), (N_SEQ * QB_DEV, KVH, TOPK), 0, 10) < 6
    others = jax.random.randint(jax.random.fold_in(key, 14), (N_SEQ * QB_DEV, KVH, TOPK), 0, PB_DEV)
    local = jnp.where(favour, popular[owners], others)
    return (local * N_SEQ + owners).astype(jnp.int32)


def block_levels(key, shape, pieces, low, largest):
    gain = 1.0
    for dim, blocks in pieces:
        steps = jax.random.uniform(jax.random.fold_in(jax.random.fold_in(key, 6), dim), (blocks,), jnp.float32, low / len(pieces), largest / len(pieces))
        gain = gain * jnp.repeat(jnp.exp(steps), shape[dim] // blocks).reshape((-1,) + (1,) * (len(shape) - 1 - dim))
    return gain


def normal_values(rng, shape, scale, reach, cuts=(), kind=jnp.bfloat16):
    array = jax.random.normal(rng, shape, jnp.float32) * scale
    if len(cuts) > 0:
        array = block_levels(rng, shape, cuts, -0.22, 0.18) * array
    return jnp.clip(array, min=-reach, max=reach).astype(kind)


def setup_inputs(seed: int = 0) -> dict:
    arg_keys = jax.random.split(jax.random.key(seed), 7)
    queries = draw_queries(jax.random.fold_in(arg_keys[6], 71), 0)
    span_keys = normal_values(arg_keys[1], (QTOK, KVH * HD), 1.0, 6.0, ((0, 128),))
    span_values = normal_values(arg_keys[2], (QTOK, KVH * HD), 1.0, 6.0, ((0, 128),))
    past_keys = draw_past_keys(jax.random.fold_in(arg_keys[6], 71), 0)
    past_values = normal_values(arg_keys[4], (PB_DEV, N_SEQ, BLOCK, KVH * HD), 1.0, 6.0, ((1, 128),))
    selected = draw_selected(jax.random.fold_in(arg_keys[6], 71), 0)
    return dict(queries=queries, span_keys=span_keys, span_values=span_values, past_keys=past_keys, past_values=past_values, selected=selected)


def reference(queries, span_keys, span_values, past_keys, past_values, selected):
    group = QH // KVH
    scale = HD ** -0.5
    blocks_all = QB_DEV * N_SEQ
    query_blocks = queries.reshape(blocks_all, BLOCK, KVH, group, HD)
    near_keys_all = span_keys.reshape(blocks_all, BLOCK, KVH, HD)
    near_values_all = span_values.reshape(blocks_all, BLOCK, KVH, HD)
    far_keys_all = past_keys.reshape(PB_DEV * N_SEQ, BLOCK, KVH, HD)
    far_values_all = past_values.reshape(PB_DEV * N_SEQ, BLOCK, KVH, HD)
    head_ids = jnp.arange(KVH, dtype=jnp.int32)[:, None]
    causal = jnp.arange(BLOCK)[None, :] <= jnp.arange(BLOCK)[:, None]

    def one_block(items):
        query_block, near_keys, near_values, chosen = items
        far_keys = far_keys_all[chosen, :, head_ids, :].reshape(KVH, TOPK * BLOCK, HD).astype(jnp.float32)
        far_values = far_values_all[chosen, :, head_ids, :].reshape(KVH, TOPK * BLOCK, HD).astype(jnp.float32)
        query_wide = query_block.astype(jnp.float32)
        far = jnp.einsum("ihgd,hkd->hgik", query_wide, far_keys) * scale
        near = jnp.einsum("ihgd,jhd->hgij", query_wide, near_keys.astype(jnp.float32)) * scale
        near = jnp.where(causal, near, -jnp.inf)
        top = jnp.maximum(jnp.max(far, axis=-1), jnp.max(near, axis=-1))[..., None]
        far_weight = jnp.exp(far - top)
        near_weight = jnp.exp(near - top)
        total = jnp.sum(far_weight, axis=-1, keepdims=True) + jnp.sum(near_weight, axis=-1, keepdims=True)
        far_probs = (far_weight / total).astype(jnp.bfloat16).astype(jnp.float32)
        near_probs = (near_weight / total).astype(jnp.bfloat16).astype(jnp.float32)
        result = jnp.einsum("hgik,hkd->ihgd", far_probs, far_values)
        result = result + jnp.einsum("hgij,jhd->ihgd", near_probs, near_values.astype(jnp.float32))
        return result.astype(jnp.bfloat16).reshape(BLOCK, QH * HD)

    attended = lax.map(one_block, (query_blocks, near_keys_all, near_values_all, selected))
    return attended.reshape(blocks_all * BLOCK, QH * HD)
```

```python
import functools
import jax
import jax.numpy as jnp
from jax import lax
from jax.experimental import pallas as pl
from jax.experimental.pallas import tpu as pltpu
from jax.sharding import PartitionSpec as P

BLOCK, HD, GROUP, TOPK = 512, 128, 4, 4
SHIFT = 1024


def segments(start, rows):
    out = []
    if start < BLOCK:
        n = min(rows, BLOCK - start)
        out.append((0, n, 0, start))
        if rows > n:
            out.append((n, rows - n, 1, 0))
    else:
        out.append((0, rows, 1, start - BLOCK))
    return out


def attend_kernel(pieces, counts, table, q_ref, nk_ref, nv_ref, *refs):
    total = sum(counts)
    sources = refs[:total]
    out_ref, k_buf, v_buf, nv_buf, sems = refs[total:]
    step = pl.program_id(0)
    steps = pl.num_programs(0)
    scale = HD ** -0.5 * 1.4426950408889634

    def fetch(g, slot):
        for j in range(TOPK):
            base = 0
            for p, (start, rows) in enumerate(pieces):
                where = table[p, g * TOPK + j]
                which = where // SHIFT
                row = where - which * SHIFT
                for n in range(counts[p]):
                    def go(ref=sources[base + n]):
                        for s0, length, kind, d0 in segments(start, rows):
                            if kind == 0:
                                dst = k_buf.at[slot, j, pl.ds(d0, length), :]
                            else:
                                dst = v_buf.at[slot, j, pl.ds(d0, length), pl.ds(0, HD)]
                            pltpu.make_async_copy(
                                ref.at[row, pl.ds(s0, length), :], dst, sems.at[slot]
                            ).start()
                    if counts[p] == 1:
                        go()
                    else:
                        pl.when(which == n)(go)
                base += counts[p]

    slot = lax.rem(step, 2)

    @pl.when(step == 0)
    def _():
        v_buf[:, :, :, HD:] = jnp.ones((2, TOPK, BLOCK, HD), jnp.bfloat16)
        nv_buf[:, HD:] = jnp.ones((BLOCK, HD), jnp.bfloat16)
        fetch(0, 0)

    @pl.when(step + 1 < steps)
    def _():
        fetch(step + 1, 1 - slot)

    nv_buf[:, :HD] = nv_ref[...]
    pltpu.make_async_copy(k_buf.at[slot], k_buf.at[slot], sems.at[slot]).wait()
    pltpu.make_async_copy(
        k_buf.at[slot], v_buf.at[slot, :, :, pl.ds(0, HD)], sems.at[slot]
    ).wait()

    half = 256
    for a in range(GROUP):
        for part in range(2):
            keys = half * (part + 1)
            q = q_ref[pl.ds(part * half, half), pl.ds(a * HD, HD)]
            dims = (((1,), (1,)), ((), ()))
            scores = [
                lax.dot_general(q, k_buf[slot, j], dims, preferred_element_type=jnp.float32)
                for j in range(TOPK)
            ]
            near = lax.dot_general(q, nk_ref[:keys, :], dims, preferred_element_type=jnp.float32)
            seen = lax.broadcasted_iota(jnp.int32, (half, keys), 1) <= (
                lax.broadcasted_iota(jnp.int32, (half, keys), 0) + part * half
            )
            near = jnp.where(seen, near, -jnp.inf)
            top = jnp.max(near, axis=1, keepdims=True)
            for s in scores:
                top = jnp.maximum(top, jnp.max(s, axis=1, keepdims=True))
            top = top * scale
            acc = jnp.dot(
                jnp.exp2(near * scale - top).astype(jnp.bfloat16),
                nv_buf[:keys, :],
                preferred_element_type=jnp.float32,
            )
            for j in range(TOPK):
                acc += jnp.dot(
                    jnp.exp2(scores[j] * scale - top).astype(jnp.bfloat16),
                    v_buf[slot, j],
                    preferred_element_type=jnp.float32,
                )
            out_ref[pl.ds(part * half, half), pl.ds(a * HD, HD)] = (
                acc[:, :HD] / acc[:, HD:]
            ).astype(jnp.bfloat16)


def attend(queries, span_keys, span_values, table, pieces, groups):
    tokens, width = queries.shape
    heads = span_keys.shape[1] // HD
    blocks = tokens // BLOCK
    counts = [len(g) for g in groups]
    flat = [s for g in groups for s in g]
    steps = blocks * heads
    place = lambda g, t: (g // heads, lax.rem(g, heads))
    keys = BLOCK * (TOPK + 1)
    return pl.pallas_call(
        functools.partial(attend_kernel, pieces, counts),
        out_shape=jax.ShapeDtypeStruct((tokens, width), jnp.bfloat16),
        grid_spec=pltpu.PrefetchScalarGridSpec(
            num_scalar_prefetch=1,
            grid=(steps,),
            in_specs=[
                pl.BlockSpec((BLOCK, GROUP * HD), place),
                pl.BlockSpec((BLOCK, HD), place),
                pl.BlockSpec((BLOCK, HD), place),
            ]
            + [pl.BlockSpec(memory_space=pl.ANY)] * len(flat),
            out_specs=pl.BlockSpec((BLOCK, GROUP * HD), place),
            scratch_shapes=[
                pltpu.VMEM((2, TOPK, BLOCK, HD), jnp.bfloat16),
                pltpu.VMEM((2, TOPK, BLOCK, 2 * HD), jnp.bfloat16),
                pltpu.VMEM((BLOCK, 2 * HD), jnp.bfloat16),
                pltpu.SemaphoreType.DMA((2,)),
            ],
        ),
        compiler_params=pltpu.CompilerParams(
            dimension_semantics=("arbitrary",), vmem_limit_bytes=48 * 1024 * 1024
        ),
        cost_estimate=pl.CostEstimate(
            flops=4 * tokens * width * keys,
            transcendentals=tokens * (width // HD) * keys,
            bytes_accessed=50 * 1024 * 1024,
        ),
        name="attend",
    )(table, queries, span_keys, span_values, *flat)


def shards(queries, span_keys, span_values, past_keys, past_values, selected):
    count = lax.axis_size("seq")
    heads = selected.shape[1]
    chosen = selected.reshape(-1)
    owners = chosen % count
    head_flat = lax.broadcasted_iota(jnp.int32, selected.shape, 1).reshape(-1)
    wanted = chosen // count * heads + head_flat + 1
    match = owners[None, :] == jnp.arange(count, dtype=jnp.int32)[:, None]
    outgoing = jnp.sum(jnp.where(match, wanted[None, :], 0), axis=1).reshape(count, 1)
    incoming = lax.all_to_all(outgoing, "seq", split_axis=0, concat_axis=0, tiled=True)
    item = jnp.maximum(incoming.reshape(-1) - 1, 0)
    stacked = jnp.concatenate(
        [
            x.reshape(-1, BLOCK, heads, HD).transpose(0, 2, 1, 3).reshape(-1, BLOCK, HD)
            for x in (past_keys, past_values)
        ],
        axis=1,
    )
    arrived = lax.all_to_all(stacked[item], "seq", split_axis=0, concat_axis=0, tiled=True)
    return attend(
        queries, span_keys, span_values, owners[None, :], [(0, 2 * BLOCK)], [[arrived]]
    )


def solution(mesh):
    return jax.shard_map(
        shards,
        mesh=mesh,
        in_specs=(
            P("seq", None),
            P("seq", None),
            P("seq", None),
            P(None, "seq", None, None),
            P(None, "seq", None, None),
            P("seq", None, None),
        ),
        out_specs=P("seq", None),
        check_vma=False,
    )
```

```python
import functools
import jax
import jax.numpy as jnp
from jax import lax
from jax.experimental import pallas as pl
from jax.experimental.pallas import tpu as pltpu
from jax.sharding import PartitionSpec as P

BLOCK, HD, GROUP, TOPK = 512, 128, 4, 4
SHIFT = 1024


def segments(start, rows):
    out = []
    if start < BLOCK:
        n = min(rows, BLOCK - start)
        out.append((0, n, 0, start))
        if rows > n:
            out.append((n, rows - n, 1, 0))
    else:
        out.append((0, rows, 1, start - BLOCK))
    return out


def pick(which, refs, go):
    if len(refs) == 1:
        go(refs[0])
        return
    half = len(refs) // 2

    @pl.when(which < half)
    def _():
        pick(which, refs[:half], go)

    @pl.when(which >= half)
    def _():
        pick(which - half, refs[half:], go)


def attend_kernel(pieces, counts, spans, table, q_ref, nk_ref, nv_ref, *refs):
    total = sum(counts)
    sources = refs[:total]
    out_ref, k_buf, v_buf, nv_buf, sems = refs[-5:]
    heads, first, many = spans
    step = pl.program_id(0)
    steps = pl.num_programs(0)
    scale = HD ** -0.5 * 1.4426950408889634

    def fetch(g, slot):
        def one(j, _):
            base = 0
            for p, (start, rows) in enumerate(pieces):
                where = table[p * 8 + 4, (g // many * heads + first + lax.rem(g, many)) * TOPK + j]
                which = where // SHIFT
                row = where - which * SHIFT

                def go(ref, start=start, rows=rows, row=row):
                    for s0, length, kind, d0 in segments(start, rows):
                        if kind == 0:
                            dst = k_buf.at[slot, j, pl.ds(d0, length), :]
                        else:
                            dst = v_buf.at[slot, j, pl.ds(d0, length), pl.ds(0, HD)]
                        pltpu.make_async_copy(
                            ref.at[row, pl.ds(s0, length), :], dst, sems.at[slot]
                        ).start()

                pick(which, sources[base : base + counts[p]], go)
                base += counts[p]
            return 0

        lax.fori_loop(0, TOPK, one, 0)

    slot = lax.rem(step, 2)

    @pl.when(step == 0)
    def _():
        v_buf[:, :, :, HD:] = jnp.ones((2, TOPK, BLOCK, HD), jnp.bfloat16)
        nv_buf[:, HD:] = jnp.ones((BLOCK, HD), jnp.bfloat16)
        fetch(0, 0)

    @pl.when(step + 1 < steps)
    def _():
        fetch(step + 1, 1 - slot)

    nv_buf[:, :HD] = nv_ref[...]
    pltpu.make_async_copy(k_buf.at[slot], k_buf.at[slot], sems.at[slot]).wait()
    pltpu.make_async_copy(
        k_buf.at[slot], v_buf.at[slot, :, :, pl.ds(0, HD)], sems.at[slot]
    ).wait()

    half = 256
    dims = (((1,), (1,)), ((), ()))
    tiles = [(a, part) for a in range(GROUP) for part in range(BLOCK // half)]

    def score(n):
        a, part = tiles[n]
        keys = half * (part + 1)
        q = q_ref[pl.ds(part * half, half), pl.ds(a * HD, HD)]
        near = lax.dot_general(q, nk_ref[:keys, :], dims, preferred_element_type=jnp.float32)
        seen = lax.broadcasted_iota(jnp.int32, (half, keys), 1) <= (
            lax.broadcasted_iota(jnp.int32, (half, keys), 0) + part * half
        )
        out = [jnp.where(seen, near, -jnp.inf)]
        for j in range(TOPK):
            out.append(lax.dot_general(q, k_buf[slot, j], dims, preferred_element_type=jnp.float32))
        return out

    def finish(n, scores):
        a, part = tiles[n]
        keys = half * (part + 1)
        wide = None
        for x in scores:
            for m in range(x.shape[1] // HD):
                y = x[:, m * HD : (m + 1) * HD]
                wide = y if wide is None else jnp.maximum(wide, y)
        top = jnp.max(wide, axis=1, keepdims=True)
        top = top * scale
        values = [nv_buf[:keys, :]] + [v_buf[slot, j] for j in range(TOPK)]
        acc = None
        for x, v in zip(scores, values):
            w = jnp.exp2(x * scale - top).astype(jnp.bfloat16)
            y = jnp.dot(w, v, preferred_element_type=jnp.float32)
            acc = y if acc is None else acc + y
        out_ref[pl.ds(part * half, half), pl.ds(a * HD, HD)] = (
            acc[:, :HD] / acc[:, HD:]
        ).astype(jnp.bfloat16)

    held = score(0)
    for n in range(len(tiles)):
        later = score(n + 1) if n + 1 < len(tiles) else None
        finish(n, held)
        held = later


def attend(queries, span_keys, span_values, table, pieces, groups, first, many, before=None):
    tokens, width = queries.shape
    heads = span_keys.shape[1] // HD
    blocks = tokens // BLOCK
    counts = [len(g) for g in groups]
    flat = [s for g in groups for s in g]
    steps = blocks * many
    place = lambda g, t: (g // many, first + lax.rem(g, many))
    pairs = 2 * tokens * many * GROUP * BLOCK * (TOPK + 1)
    extra = [] if before is None else [before]
    return pl.pallas_call(
        functools.partial(attend_kernel, pieces, counts, (heads, first, many)),
        out_shape=jax.ShapeDtypeStruct((tokens, width), jnp.bfloat16),
        grid_spec=pltpu.PrefetchScalarGridSpec(
            num_scalar_prefetch=1,
            grid=(steps,),
            in_specs=[
                pl.BlockSpec((BLOCK, GROUP * HD), place),
                pl.BlockSpec((BLOCK, HD), place),
                pl.BlockSpec((BLOCK, HD), place),
            ]
            + [pl.BlockSpec(memory_space=pltpu.HBM)] * (len(flat) + len(extra)),
            out_specs=pl.BlockSpec((BLOCK, GROUP * HD), place),
            scratch_shapes=[
                pltpu.VMEM((2, TOPK, BLOCK, HD), jnp.bfloat16),
                pltpu.VMEM((2, TOPK, BLOCK, 2 * HD), jnp.bfloat16),
                pltpu.VMEM((BLOCK, 2 * HD), jnp.bfloat16),
                pltpu.SemaphoreType.DMA((2,)),
            ],
        ),
        input_output_aliases={} if before is None else {4 + len(flat): 0},
        compiler_params=pltpu.CompilerParams(
            dimension_semantics=("arbitrary",), vmem_limit_bytes=40 * 1024 * 1024
        ),
        cost_estimate=pl.CostEstimate(
            flops=4 * HD * pairs,
            transcendentals=pairs,
            bytes_accessed=6 * 1024 * 1024 * many,
        ),
        name="attend",
    )(table, queries, span_keys, span_values, *flat, *extra)


N = 128
STRIDE = (32, 8, 2)
ROWS = (352, 336, 336)
ITEMS = 16


def items_kernel(k_ref, v_ref, *outs):
    for n in range(4):
        lanes = pl.ds(n * HD, HD)
        start = 0
        for out, rows in zip(outs, ROWS):
            for s0, length, kind, d0 in segments(start, rows):
                ref = k_ref if kind == 0 else v_ref
                out[n, pl.ds(s0, length), :] = ref[0, 0, pl.ds(d0, length), lanes]
            start += rows


def cut_items(past_keys, past_values):
    spec = pl.BlockSpec((1, 1, BLOCK, 4 * HD), lambda p, n: (p, 0, 0, n))
    return pl.pallas_call(
        items_kernel,
        grid=(2, 2),
        in_specs=[spec, spec],
        out_specs=[pl.BlockSpec((4, r, HD), lambda p, n: (p * 2 + n, 0, 0)) for r in ROWS],
        out_shape=[jax.ShapeDtypeStruct((ITEMS, r, HD), jnp.bfloat16) for r in ROWS],
        name="cut_items",
    )(past_keys, past_values)


def plan_kernel(cut, caps2, caps3, place, w_ref, req_ref, out_ref):
    f32, bf16, i32 = jnp.float32, jnp.bfloat16, jnp.int32
    c = place[3]
    s = 1 - 2 * c
    wanted = w_ref[...].astype(f32).astype(bf16)
    lane = lax.broadcasted_iota(i32, (1, N), 1)
    sub = lax.broadcasted_iota(i32, (N, N), 0)
    lanes = lax.broadcasted_iota(i32, (N, N), 1)
    sub8 = lax.broadcasted_iota(i32, (8, N), 0)
    lane8 = lax.broadcasted_iota(i32, (8, N), 1)
    below = jnp.where(sub < lanes, 1.0, 0.0).astype(bf16)

    def mm(a, b):
        return jnp.dot(a.astype(bf16), b.astype(bf16), preferred_element_type=f32)

    def hot(row):
        return jnp.where(sub == row, 1.0, 0.0).astype(bf16)

    def stack(rows):
        out = jnp.zeros((8, N), rows[0].dtype)
        for n, row in enumerate(rows):
            out = jnp.where(sub8 == n, row, out)
        return out

    def spread(rows, chosen):
        codes = stack([r.astype(f32) for r in rows]).astype(bf16)
        out = lax.dot_general(
            codes,
            jnp.where(chosen, 1.0, 0.0).astype(bf16),
            (((1,), (1,)), ((), ())),
            preferred_element_type=f32,
        ).astype(i32)
        return out[0:1] * SHIFT + out[1:2]

    def ranked(needs, early):
        low = needs * early
        high = needs - low
        after = jnp.sum(low, axis=1, keepdims=True)
        return jnp.where(early > 0.5, mm(low, below), mm(high, below) + after)

    def seat(rank, turn, caps, base_a, base_b):
        na, nb = caps
        late = jnp.where(rank >= na, 1, 0)
        here = rank - late * na
        limit = jnp.where(late == 1, nb // 2, na // 2)
        half = jnp.where(here >= limit, 1, 0)
        buf = jnp.where(turn == 3, 0, jnp.where(turn == 1, 1, jnp.where(half == c, 2, 3)))
        pos = jnp.where(turn == 2, here - half * limit, here)
        return buf + jnp.where(late == 1, base_b, base_a), pos

    def seats(caps, late, rank_near, need_near, rank_far, need_far):
        skip = caps[0] if late else 0
        cap = caps[1] if late else caps[0]
        near_side = jnp.where((rank_near == sub + skip) & (sub < cap), need_near, 0.0) > 0.5
        far_side = (
            jnp.where(
                (rank_far == sub - cap + c * (cap // 2) + skip) & (sub >= cap) & (sub < cap + cap // 2),
                need_far,
                0.0,
            )
            > 0.5
        )
        return near_side, far_side

    for t in range(3):
        a1, a2, a3 = t, (t + 1) % 3, (t + 2) % 3
        s1, s2, s3 = STRIDE[a1], STRIDE[a2], STRIDE[a3]
        at1, at2, at3 = place[a1], place[a2], place[a3]

        o1, oc, item = lane >> 5, (lane >> 4) & 1, lane & 15
        rows = []
        for v in (at2, (at2 + s) & 3, (at2 + 2) & 3):
            who = at1 * s1 + v * s2 + (sub8 >> 1) * s3 + (sub8 & 1)
            rows.append(mm(jnp.where(lane8 == who, 1.0, 0.0), wanted))
        needs = []
        for q in range(4):
            got = mm(rows[0], hot(o1 * s1 + q * s2 + at3 * s3 + oc))
            needs.append(jnp.max(jnp.where(got.astype(i32) == item + 1, 1.0, 0.0), axis=0, keepdims=True))
        mine = hot(o1 * s1 + at2 * s2 + at3 * s3 + oc)
        for n in (1, 2):
            got = mm(rows[n], mine)
            needs.append(jnp.max(jnp.where(got.astype(i32) == item + 1, 1.0, 0.0), axis=0, keepdims=True))
        needs2 = stack(needs)
        rank2 = ranked(needs2, jnp.where((lane8 & 7) < cut, 1.0, 0.0))
        ranks2 = rank2.astype(i32)

        def first(b1, bc, bi):
            r1 = ((b1 - at1) * s) & 3
            same = bc == c
            buf = jnp.where(r1 == 0, jnp.where(same, 0, 1), jnp.where(r1 == 3, jnp.where(same, 2, 3), jnp.where(r1 == 1, jnp.where(same, 5, 4), jnp.where(same, 6, 7))))
            return buf, bi

        def second(b1, b2, bc, bi):
            buf, pos = first(b1, bc, bi)
            found = mm(rank2, hot((b1 * 2 + bc) * ITEMS + bi)).astype(i32)
            rank = jnp.zeros((1, N), i32)
            for q in range(4):
                rank = jnp.where(b2 == q, found[q : q + 1], rank)
            r2 = ((b2 - at2) * s) & 3
            far_buf, far_pos = seat(rank, r2, caps2, 8, 12)
            return jnp.where(r2 == 0, buf, far_buf), jnp.where(r2 == 0, pos, far_pos)

        packed = []
        for late in (0, 1):
            near_side, far_side = seats(
                caps2, late, ranks2[4:5], needs2[4:5], ranks2[5:6], needs2[5:6]
            )
            packed.append(spread(first(o1, oc, item), near_side | far_side))

        rc, o1, o2, oc = lane >> 5, (lane >> 3) & 3, (lane >> 1) & 3, lane & 1
        turn = sub8 >> 1
        v = jnp.where(turn == 0, at3, jnp.where(turn == 1, (at3 + s) & 3, (at3 + 2) & 3))
        who = jnp.where(sub8 < 6, at1 * s1 + at2 * s2 + v * s3 + (sub8 & 1), -1)
        asked = mm(jnp.where(lane8 == who, 1.0, 0.0), wanted)
        values = []
        for q in range(4):
            got = mm(asked, hot(o1 * s1 + o2 * s2 + q * s3 + oc))
            values.append(jnp.where(rc == 0, got[0:1], got[1:2]))
        got = mm(asked, hot(o1 * s1 + o2 * s2 + at3 * s3 + oc))
        values.append(jnp.where(rc == 0, got[2:3], got[3:4]))
        values.append(jnp.where(rc == 0, got[4:5], got[5:6]))
        values = stack(values)
        needs3 = jnp.where((values > 0.5) & (lane8 < 64), 1.0, 0.0)
        which = jnp.maximum(values.astype(i32) - 1, 0)
        rank3 = ranked(needs3, jnp.where((which & 7) < cut, 1.0, 0.0))
        ranks3 = rank3.astype(i32)
        for late in (0, 1):
            near_side, far_side = seats(
                caps3, late, ranks3[4:5], needs3[4:5], ranks3[5:6], needs3[5:6]
            )
            packed.append(
                spread(second(o1, o2, oc, which[4:5]), near_side)
                + spread(second(o1, o2, oc, which[5:6]), far_side)
            )

        owner, item = req_ref[0:1, :], req_ref[1:2, :]
        digit = lambda stride: (owner >> (stride.bit_length() - 1)) & 3
        o1, o2, o3, oc = digit(s1), digit(s2), digit(s3), owner & 1
        buf, pos = second(o1, o2, oc, item)
        found = mm(rank3, hot(c * 32 + o1 * 8 + o2 * 2 + oc)).astype(i32)
        rank = jnp.zeros((1, N), i32)
        for q in range(4):
            rank = jnp.where(o3 == q, found[q : q + 1], rank)
        r3 = ((o3 - at3) * s) & 3
        far_buf, far_pos = seat(rank, r3, caps3, jnp.where((item & 7) < cut, 12, 16), 20)
        final = jnp.where(r3 == 0, buf, far_buf) * SHIFT + jnp.where(r3 == 0, pos, far_pos)
        out_ref[pl.ds(t * 8, 8), :] = stack([*packed, final])


def check_kernel(cut, w_ref, out_ref):
    f32, bf16, i32 = jnp.float32, jnp.bfloat16, jnp.int32
    wanted = w_ref[...]
    digit = lambda x, stride: (x >> (stride.bit_length() - 1)) & 3
    row48 = lax.broadcasted_iota(i32, (48, N), 0)
    lane48 = lax.broadcasted_iota(i32, (48, N), 1)
    sub = lax.broadcasted_iota(i32, (N, N), 0)
    lanes = lax.broadcasted_iota(i32, (N, N), 1)

    def mm(a, b):
        return jnp.dot(a.astype(bf16), b.astype(bf16), preferred_element_type=f32)

    groups = jnp.zeros((48, N), f32)
    for t in range(3):
        s1, s2 = STRIDE[t], STRIDE[(t + 1) % 3]
        hit = row48 == t * 16 + digit(lane48, s1) * 4 + digit(lane48, s2)
        groups = jnp.where(hit, 1.0, groups)
    sums = [jnp.zeros((48, N), f32), jnp.zeros((48, N), f32)]
    for n in range(ITEMS):
        any_wants = mm(groups, jnp.where(wanted == n + 1, 1.0, 0.0)) > 0.5
        late = 0 if (n & 7) < cut else 1
        sums[late] += jnp.where(any_wants, 1.0, 0.0)
    early2, all2 = jnp.zeros((48, N), f32), jnp.zeros((48, N), f32)
    for t in range(3):
        s2, s3 = STRIDE[(t + 1) % 3], STRIDE[(t + 2) % 3]
        owners = jnp.where(lanes == digit(sub, s2) * 4 + digit(sub, s3), 1.0, 0.0)
        keep = (row48 >> 4 == t) & ((row48 & 3) != (lane48 >> 2)) & (lane48 < 16)
        early = mm(sums[0], owners)
        early2 = jnp.where(keep, early, early2)
        all2 = jnp.where(keep, early + mm(sums[1], owners), all2)
    chip = lax.broadcasted_iota(i32, (64, N), 0)
    lane64 = lax.broadcasted_iota(i32, (64, N), 1)
    pairs = jnp.where(lane64 >> 1 == chip, 1.0, 0.0)
    low = jnp.where((wanted > 0) & (((wanted - 1) & 7) < cut), 1.0, 0.0)
    every = jnp.where(wanted > 0, 1.0, 0.0)
    owners = jnp.zeros((N, N), f32)
    keep = lane64 < 12
    for t in range(3):
        s3 = STRIDE[(t + 2) % 3]
        owners = jnp.where(lanes == t * 4 + digit(sub, s3), 1.0, owners)
        keep = keep & (lane64 != t * 4 + digit(chip * 2, s3))
    early3 = jnp.where(keep, mm(mm(pairs, low), owners), 0.0)
    all3 = jnp.where(keep, mm(mm(pairs, every), owners), 0.0)
    out = jnp.zeros((8, N), f32)
    sub8 = lax.broadcasted_iota(i32, (8, N), 0)
    for n, x in enumerate((early2, all2, early3, all3)):
        top = jnp.max(jnp.max(x, axis=1, keepdims=True), axis=0, keepdims=True)
        out = jnp.where(sub8 == n, top, out)
    out_ref[...] = out.astype(i32)


def longest(cut, wanted):
    return pl.pallas_call(
        functools.partial(check_kernel, cut),
        out_shape=jax.ShapeDtypeStruct((8, N), jnp.int32),
        in_specs=[pl.BlockSpec(memory_space=pltpu.VMEM)],
        out_specs=pl.BlockSpec(memory_space=pltpu.VMEM),
        name="longest",
    )(wanted)


def make_plan(cut, caps2, caps3, place, wanted, requests):
    return pl.pallas_call(
        functools.partial(plan_kernel, cut, caps2, caps3),
        out_shape=jax.ShapeDtypeStruct((24, N), jnp.int32),
        grid_spec=pltpu.PrefetchScalarGridSpec(
            num_scalar_prefetch=1,
            grid=(1,),
            in_specs=[
                pl.BlockSpec((N, N), lambda i, t: (0, 0)),
                pl.BlockSpec((8, N), lambda i, t: (0, 0)),
            ],
            out_specs=pl.BlockSpec((24, N), lambda i, t: (0, 0)),
        ),
        name="plan",
    )(place, wanted, requests)


def pack_kernel(row, first, count, n_sources, table, *refs):
    sources, out, sem = refs[:n_sources], refs[n_sources], refs[n_sources + 1]

    def one(k, _):
        where = table[row, first + k]
        which = where // SHIFT
        pos = where - which * SHIFT
        pick(which, sources, lambda ref: pltpu.make_async_copy(ref.at[pos], out.at[k], sem).start())
        return 0

    lax.fori_loop(0, count, one, 0)
    pltpu.make_async_copy(out, out, sem).wait()


def pack(table, row, first, count, sources):
    rows = sources[0].shape[1]
    return pl.pallas_call(
        functools.partial(pack_kernel, row, first, count, len(sources)),
        out_shape=jax.ShapeDtypeStruct((count, rows, HD), jnp.bfloat16),
        in_specs=[pl.BlockSpec(memory_space=pltpu.SMEM)]
        + [pl.BlockSpec(memory_space=pltpu.HBM)] * len(sources),
        out_specs=pl.BlockSpec(memory_space=pltpu.VMEM),
        scratch_shapes=[pltpu.SemaphoreType.DMA],
        compiler_params=pltpu.CompilerParams(vmem_limit_bytes=24 * 1024 * 1024),
        name="pack",
    )(table, *sources)


def ring_pairs(axis):
    pairs = []
    for i in range(N):
        at = (i // STRIDE[axis]) % 4
        to = (at + (1 if i % 2 == 0 else 3)) % 4
        pairs.append((i, i + (to - at) * STRIDE[axis]))
    return pairs


def onward(x, axis):
    return lax.ppermute(x, "seq", ring_pairs(axis))


def swap(x):
    return lax.ppermute(x, "seq", [(i, i ^ 1) for i in range(N)])


def hop(pools, table, row, axis_of, cap):
    half = cap // 2
    packed = [pack(table, t * 8 + row, cap, half, pools[t]) for t in range(3)]
    table, packed = lax.optimization_barrier((table, packed))
    through = [onward(packed[t], axis_of(t)) for t in range(3)]
    direct = [onward(pack(table, t * 8 + row, 0, cap, pools[t]), axis_of(t)) for t in range(3)]
    passed = [onward(through[t], axis_of(t)) for t in range(3)]
    return [[direct[t], swap(direct[t]), passed[t], swap(passed[t])] for t in range(3)]


def join(*lists):
    return [sum((x[t] for x in lists), []) for t in range(3)]


def route(cut, caps2, caps3, splits, queries, span_keys, span_values, pools, place, wanted, requests, table):
    if caps2 != FAST[1]:
        table = make_plan(cut, caps2, caps3, place, wanted, requests)
    side = lambda t: (t + 1) % 3
    last = lambda t: (t + 2) % 3
    starts = (0, ROWS[0], ROWS[0] + ROWS[1])
    pieces = list(zip(starts, ROWS))
    two_a = hop(pools, table, 0, side, caps2[0])
    three_a = hop(join(pools, two_a), table, 2, last, caps3[0])
    groups = [join(pools, two_a, three_a)]
    if caps2[1]:
        two_b = hop(pools, table, 1, side, caps2[1])
        three_b = hop(join(pools, two_a, two_b), table, 3, last, caps3[1])
        groups.append(join(pools, two_a, two_b, three_a, three_b))
    out = None
    for ranges, found in zip(splits, groups):
        for first, many in ranges:
            out = attend(queries, span_keys, span_values, table, pieces, found, first, many, out)
    return out


FAST = (8, (44, 0), (48, 0), (((0, 8),),))
SAFE = (8, (64, 0), (64, 0), (((0, 8),),))


def shards(queries, span_keys, span_values, past_keys, past_values, selected):
    heads = selected.shape[1]
    me = lax.axis_index("seq")
    place = jnp.stack([me // 32, me // 8 % 4, me // 2 % 4, me % 2]).astype(jnp.int32)
    chosen = selected.reshape(-1)
    owners = chosen % N
    item = chosen // N * heads + lax.broadcasted_iota(jnp.int32, selected.shape, 1).reshape(-1)
    match = owners[None, :] == jnp.arange(N, dtype=jnp.int32)[:, None]
    outgoing = jnp.sum(jnp.where(match, item[None, :] + 1, 0), axis=1)
    copies = jnp.broadcast_to(outgoing, (N, 1, N))
    wanted = lax.all_to_all(copies, "seq", split_axis=0, concat_axis=0, tiled=True).reshape(N, N)
    requests = jnp.pad(jnp.stack([owners, item]), ((0, 6), (0, N - owners.shape[0])))

    own = cut_items(past_keys, past_values)
    ahead = [onward(own[t], t) for t in range(3)]
    raw = [swap(past_keys), swap(past_values)]
    raw, wanted = lax.optimization_barrier((raw, wanted))
    mate = cut_items(*raw)
    ahead_mate = [onward(mate[t], t) for t in range(3)]
    table = make_plan(*FAST[:3], place, wanted, requests)
    most = longest(FAST[0], wanted)[:4, 0]
    fits = jnp.all(most <= jnp.array([FAST[1][0], sum(FAST[1]), FAST[2][0], sum(FAST[2])]))
    ahead, table, fits = lax.optimization_barrier((ahead, table, fits))
    twice = [onward(ahead[t], t) for t in range(3)]
    pools = [
        [own[t], mate[t], ahead[t], ahead_mate[t], swap(ahead[t]), swap(ahead_mate[t]), twice[t], swap(twice[t])]
        for t in range(3)
    ]
    args = (queries, span_keys, span_values, pools, place, wanted, requests, table)
    return lax.cond(
        fits, functools.partial(route, *FAST), functools.partial(route, *SAFE), *args
    )


def solution(mesh):
    return jax.shard_map(
        shards,
        mesh=mesh,
        in_specs=(
            P("seq", None),
            P("seq", None),
            P("seq", None),
            P(None, "seq", None, None),
            P(None, "seq", None, None),
            P("seq", None, None),
        ),
        out_specs=P("seq", None),
        check_vma=False,
    )
```

```python
import functools
import jax
import jax.numpy as jnp
from jax import lax
from jax.experimental import pallas as pl
from jax.experimental.pallas import tpu as pltpu
from jax.sharding import PartitionSpec as P

BLOCK, HD, GROUP, TOPK = 512, 128, 4, 4
SHIFT = 1024


def segments(start, rows):
    out = []
    if start < BLOCK:
        n = min(rows, BLOCK - start)
        out.append((0, n, 0, start))
        if rows > n:
            out.append((n, rows - n, 1, 0))
    else:
        out.append((0, rows, 1, start - BLOCK))
    return out


def pick(which, refs, go):
    if len(refs) == 1:
        go(refs[0])
        return
    half = len(refs) // 2
    lax.cond(
        which < half,
        lambda: pick(which, refs[:half], go),
        lambda: pick(which - half, refs[half:], go),
    )


def attend_kernel(pieces, counts, spans, table, q_ref, nk_ref, nv_ref, *refs):
    total = sum(counts)
    sources = refs[:total]
    out_ref, k_buf, v_buf, nv_buf, sems = refs[-5:]
    heads, first, many, unroll = spans
    step = pl.program_id(0)
    steps = pl.num_programs(0)
    scale = HD ** -0.5 * 1.4426950408889634

    def fetch(g, slot):
        def one(j, _):
            base = 0
            for p, (start, rows) in enumerate(pieces):
                where = table[p * 8 + 4, (g // many * heads + first + lax.rem(g, many)) * TOPK + j]
                which = where // SHIFT
                row = where - which * SHIFT

                def go(ref, start=start, rows=rows, row=row):
                    for s0, length, kind, d0 in segments(start, rows):
                        if kind == 0:
                            dst = k_buf.at[slot, j, pl.ds(d0, length), :]
                        else:
                            dst = v_buf.at[slot, j, pl.ds(d0, length), pl.ds(0, HD)]
                        pltpu.make_async_copy(
                            ref.at[row, pl.ds(s0, length), :], dst, sems.at[slot]
                        ).start()

                pick(which, sources[base : base + counts[p]], go)
                base += counts[p]
            return 0

        lax.fori_loop(0, TOPK, one, 0)

    slot = lax.rem(step, 2)

    @pl.when(step == 0)
    def _():
        v_buf[:, :, :, HD:] = jnp.ones((2, TOPK, BLOCK, HD), jnp.bfloat16)
        nv_buf[:, HD:] = jnp.ones((BLOCK, HD), jnp.bfloat16)
        fetch(0, 0)

    @pl.when(step + 1 < steps)
    def _():
        fetch(step + 1, 1 - slot)

    nv_buf[:, :HD] = nv_ref[...]
    pltpu.make_async_copy(k_buf.at[slot], k_buf.at[slot], sems.at[slot]).wait()
    pltpu.make_async_copy(
        k_buf.at[slot], v_buf.at[slot, :, :, pl.ds(0, HD)], sems.at[slot]
    ).wait()

    half = 256
    dims = (((1,), (1,)), ((), ()))
    parts = BLOCK // half
    head_lanes = lambda a: pl.ds(a * HD if unroll else pl.multiple_of(a * HD, HD), HD)

    def score(tile):
        a, part = tile
        keys = half * (part + 1)
        q = q_ref[pl.ds(part * half, half), head_lanes(a)]
        near = lax.dot_general(q, nk_ref[:keys, :], dims, preferred_element_type=jnp.float32)
        seen = lax.broadcasted_iota(jnp.int32, (half, keys), 1) <= (
            lax.broadcasted_iota(jnp.int32, (half, keys), 0) + part * half
        )
        out = [jnp.where(seen, near, -jnp.inf)]
        for j in range(TOPK):
            out.append(lax.dot_general(q, k_buf[slot, j], dims, preferred_element_type=jnp.float32))
        return out

    def finish(tile, scores):
        a, part = tile
        keys = half * (part + 1)
        wide = None
        for x in scores:
            for m in range(x.shape[1] // HD):
                y = x[:, m * HD : (m + 1) * HD]
                wide = y if wide is None else jnp.maximum(wide, y)
        top = jnp.max(wide, axis=1, keepdims=True)
        top = top * scale
        values = [nv_buf[:keys, :]] + [v_buf[slot, j] for j in range(TOPK)]
        acc = None
        for x, v in zip(scores, values):
            w = jnp.exp2(x * scale - top).astype(jnp.bfloat16)
            y = jnp.dot(w, v, preferred_element_type=jnp.float32)
            acc = y if acc is None else acc + y
        out_ref[pl.ds(part * half, half), head_lanes(a)] = (
            acc[:, :HD] / acc[:, HD:]
        ).astype(jnp.bfloat16)

    def chain(tiles):
        held = score(tiles[0])
        for n, tile in enumerate(tiles):
            later = score(tiles[n + 1]) if n + 1 < len(tiles) else None
            finish(tile, held)
            held = later

    if unroll:
        chain([(a, part) for a in range(GROUP) for part in range(parts)])
    else:

        @pl.loop(0, GROUP)
        def _(a):
            chain([(a, part) for part in range(parts)])


def attend(queries, span_keys, span_values, table, pieces, groups, first, many, unroll, before=None):
    tokens, width = queries.shape
    heads = span_keys.shape[1] // HD
    blocks = tokens // BLOCK
    counts = [len(g) for g in groups]
    flat = [s for g in groups for s in g]
    steps = blocks * many
    place = lambda g, t: (g // many, first + lax.rem(g, many))
    pairs = 2 * tokens * many * GROUP * BLOCK * (TOPK + 1)
    extra = [] if before is None else [before]
    return pl.pallas_call(
        functools.partial(attend_kernel, pieces, counts, (heads, first, many, unroll)),
        out_shape=jax.ShapeDtypeStruct((tokens, width), jnp.bfloat16),
        grid_spec=pltpu.PrefetchScalarGridSpec(
            num_scalar_prefetch=1,
            grid=(steps,),
            in_specs=[
                pl.BlockSpec((BLOCK, GROUP * HD), place),
                pl.BlockSpec((BLOCK, HD), place),
                pl.BlockSpec((BLOCK, HD), place),
            ]
            + [pl.BlockSpec(memory_space=pl.ANY)] * (len(flat) + len(extra)),
            out_specs=pl.BlockSpec((BLOCK, GROUP * HD), place),
            scratch_shapes=[
                pltpu.VMEM((2, TOPK, BLOCK, HD), jnp.bfloat16),
                pltpu.VMEM((2, TOPK, BLOCK, 2 * HD), jnp.bfloat16),
                pltpu.VMEM((BLOCK, 2 * HD), jnp.bfloat16),
                pltpu.SemaphoreType.DMA((2,)),
            ],
        ),
        input_output_aliases={} if before is None else {4 + len(flat): 0},
        compiler_params=pltpu.CompilerParams(
            dimension_semantics=("arbitrary",), vmem_limit_bytes=20 * 1024 * 1024
        ),
        cost_estimate=pl.CostEstimate(
            flops=4 * HD * pairs,
            transcendentals=pairs,
            bytes_accessed=6 * 1024 * 1024 * many,
        ),
        name="attend",
    )(table, queries, span_keys, span_values, *flat, *extra)


N = 128
STRIDE = (32, 8, 2)
ROWS = (352, 336, 336)
ITEMS = 16


def items_kernel(k_ref, v_ref, *outs):
    for n in range(4):
        lanes = pl.ds(n * HD, HD)
        start = 0
        for out, rows in zip(outs, ROWS):
            for s0, length, kind, d0 in segments(start, rows):
                ref = k_ref if kind == 0 else v_ref
                out[n, pl.ds(s0, length), :] = ref[0, 0, pl.ds(d0, length), lanes]
            start += rows


def cut_items(past_keys, past_values):
    spec = pl.BlockSpec((1, 1, BLOCK, 4 * HD), lambda p, n: (p, 0, 0, n))
    return pl.pallas_call(
        items_kernel,
        grid=(2, 2),
        in_specs=[spec, spec],
        out_specs=[pl.BlockSpec((4, r, HD), lambda p, n: (p * 2 + n, 0, 0)) for r in ROWS],
        out_shape=[jax.ShapeDtypeStruct((ITEMS, r, HD), jnp.bfloat16) for r in ROWS],
        name="cut_items",
    )(past_keys, past_values)


def plan_kernel(cut, caps2, caps3, place, w_ref, req_ref, out_ref):
    f32, bf16, i32 = jnp.float32, jnp.bfloat16, jnp.int32
    c = place[3]
    s = 1 - 2 * c
    wanted = w_ref[...].astype(f32).astype(bf16)
    lane = lax.broadcasted_iota(i32, (1, N), 1)
    sub = lax.broadcasted_iota(i32, (N, N), 0)
    lanes = lax.broadcasted_iota(i32, (N, N), 1)
    sub8 = lax.broadcasted_iota(i32, (8, N), 0)
    lane8 = lax.broadcasted_iota(i32, (8, N), 1)
    below = jnp.where(sub < lanes, 1.0, 0.0).astype(bf16)

    def mm(a, b):
        return jnp.dot(a.astype(bf16), b.astype(bf16), preferred_element_type=f32)

    def hot(row):
        return jnp.where(sub == row, 1.0, 0.0).astype(bf16)

    def stack(rows):
        out = jnp.zeros((8, N), rows[0].dtype)
        for n, row in enumerate(rows):
            out = jnp.where(sub8 == n, row, out)
        return out

    def spread(rows, chosen):
        codes = stack([r.astype(f32) for r in rows]).astype(bf16)
        out = lax.dot_general(
            codes,
            jnp.where(chosen, 1.0, 0.0).astype(bf16),
            (((1,), (1,)), ((), ())),
            preferred_element_type=f32,
        ).astype(i32)
        return out[0:1] * SHIFT + out[1:2]

    def ranked(needs, early):
        low = needs * early
        high = needs - low
        after = jnp.sum(low, axis=1, keepdims=True)
        return jnp.where(early > 0.5, mm(low, below), mm(high, below) + after)

    def seat(rank, turn, caps, base_a, base_b):
        na, nb = caps
        late = jnp.where(rank >= na, 1, 0)
        here = rank - late * na
        limit = jnp.where(late == 1, nb // 2, na // 2)
        half = jnp.where(here >= limit, 1, 0)
        buf = jnp.where(turn == 3, 0, jnp.where(turn == 1, 1, jnp.where(half == c, 2, 3)))
        pos = jnp.where(turn == 2, here - half * limit, here)
        return buf + jnp.where(late == 1, base_b, base_a), pos

    def seats(caps, late, rank_near, need_near, rank_far, need_far):
        skip = caps[0] if late else 0
        cap = caps[1] if late else caps[0]
        near_side = jnp.where((rank_near == sub + skip) & (sub < cap), need_near, 0.0) > 0.5
        far_side = (
            jnp.where(
                (rank_far == sub - cap + c * (cap // 2) + skip) & (sub >= cap) & (sub < cap + cap // 2),
                need_far,
                0.0,
            )
            > 0.5
        )
        return near_side, far_side

    for t in range(3):
        a1, a2, a3 = t, (t + 1) % 3, (t + 2) % 3
        s1, s2, s3 = STRIDE[a1], STRIDE[a2], STRIDE[a3]
        at1, at2, at3 = place[a1], place[a2], place[a3]

        o1, oc, item = lane >> 5, (lane >> 4) & 1, lane & 15
        rows = []
        for v in (at2, (at2 + s) & 3, (at2 + 2) & 3):
            who = at1 * s1 + v * s2 + (sub8 >> 1) * s3 + (sub8 & 1)
            rows.append(mm(jnp.where(lane8 == who, 1.0, 0.0), wanted))
        needs = []
        for q in range(4):
            got = mm(rows[0], hot(o1 * s1 + q * s2 + at3 * s3 + oc))
            needs.append(jnp.max(jnp.where(got.astype(i32) == item + 1, 1.0, 0.0), axis=0, keepdims=True))
        mine = hot(o1 * s1 + at2 * s2 + at3 * s3 + oc)
        for n in (1, 2):
            got = mm(rows[n], mine)
            needs.append(jnp.max(jnp.where(got.astype(i32) == item + 1, 1.0, 0.0), axis=0, keepdims=True))
        needs2 = stack(needs)
        rank2 = ranked(needs2, jnp.where((lane8 & 7) < cut, 1.0, 0.0))
        ranks2 = rank2.astype(i32)

        def first(b1, bc, bi):
            r1 = ((b1 - at1) * s) & 3
            same = bc == c
            buf = jnp.where(r1 == 0, jnp.where(same, 0, 1), jnp.where(r1 == 3, jnp.where(same, 2, 3), jnp.where(r1 == 1, jnp.where(same, 5, 4), jnp.where(same, 6, 7))))
            return buf, bi

        def second(b1, b2, bc, bi):
            buf, pos = first(b1, bc, bi)
            found = mm(rank2, hot((b1 * 2 + bc) * ITEMS + bi)).astype(i32)
            rank = jnp.zeros((1, N), i32)
            for q in range(4):
                rank = jnp.where(b2 == q, found[q : q + 1], rank)
            r2 = ((b2 - at2) * s) & 3
            far_buf, far_pos = seat(rank, r2, caps2, 8, 12)
            return jnp.where(r2 == 0, buf, far_buf), jnp.where(r2 == 0, pos, far_pos)

        packed = []
        for late in (0, 1):
            near_side, far_side = seats(
                caps2, late, ranks2[4:5], needs2[4:5], ranks2[5:6], needs2[5:6]
            )
            packed.append(spread(first(o1, oc, item), near_side | far_side))

        rc, o1, o2, oc = lane >> 5, (lane >> 3) & 3, (lane >> 1) & 3, lane & 1
        turn = sub8 >> 1
        v = jnp.where(turn == 0, at3, jnp.where(turn == 1, (at3 + s) & 3, (at3 + 2) & 3))
        who = jnp.where(sub8 < 6, at1 * s1 + at2 * s2 + v * s3 + (sub8 & 1), -1)
        asked = mm(jnp.where(lane8 == who, 1.0, 0.0), wanted)
        values = []
        for q in range(4):
            got = mm(asked, hot(o1 * s1 + o2 * s2 + q * s3 + oc))
            values.append(jnp.where(rc == 0, got[0:1], got[1:2]))
        got = mm(asked, hot(o1 * s1 + o2 * s2 + at3 * s3 + oc))
        values.append(jnp.where(rc == 0, got[2:3], got[3:4]))
        values.append(jnp.where(rc == 0, got[4:5], got[5:6]))
        values = stack(values)
        needs3 = jnp.where((values > 0.5) & (lane8 < 64), 1.0, 0.0)
        which = jnp.maximum(values.astype(i32) - 1, 0)
        rank3 = ranked(needs3, jnp.where((which & 7) < cut, 1.0, 0.0))
        ranks3 = rank3.astype(i32)
        for late in (0, 1):
            near_side, far_side = seats(
                caps3, late, ranks3[4:5], needs3[4:5], ranks3[5:6], needs3[5:6]
            )
            packed.append(
                spread(second(o1, o2, oc, which[4:5]), near_side)
                + spread(second(o1, o2, oc, which[5:6]), far_side)
            )

        owner, item = req_ref[0:1, :], req_ref[1:2, :]
        digit = lambda stride: (owner >> (stride.bit_length() - 1)) & 3
        o1, o2, o3, oc = digit(s1), digit(s2), digit(s3), owner & 1
        buf, pos = second(o1, o2, oc, item)
        found = mm(rank3, hot(c * 32 + o1 * 8 + o2 * 2 + oc)).astype(i32)
        rank = jnp.zeros((1, N), i32)
        for q in range(4):
            rank = jnp.where(o3 == q, found[q : q + 1], rank)
        r3 = ((o3 - at3) * s) & 3
        far_buf, far_pos = seat(rank, r3, caps3, jnp.where((item & 7) < cut, 12, 16), 20)
        final = jnp.where(r3 == 0, buf, far_buf) * SHIFT + jnp.where(r3 == 0, pos, far_pos)
        out_ref[pl.ds(t * 8, 8), :] = stack([*packed, final])


def check_kernel(cut, w_ref, out_ref):
    f32, bf16, i32 = jnp.float32, jnp.bfloat16, jnp.int32
    wanted = w_ref[...]
    digit = lambda x, stride: (x >> (stride.bit_length() - 1)) & 3
    row48 = lax.broadcasted_iota(i32, (48, N), 0)
    lane48 = lax.broadcasted_iota(i32, (48, N), 1)
    sub = lax.broadcasted_iota(i32, (N, N), 0)
    lanes = lax.broadcasted_iota(i32, (N, N), 1)

    def mm(a, b):
        return jnp.dot(a.astype(bf16), b.astype(bf16), preferred_element_type=f32)

    groups = jnp.zeros((48, N), f32)
    for t in range(3):
        s1, s2 = STRIDE[t], STRIDE[(t + 1) % 3]
        hit = row48 == t * 16 + digit(lane48, s1) * 4 + digit(lane48, s2)
        groups = jnp.where(hit, 1.0, groups)
    sums = [jnp.zeros((48, N), f32), jnp.zeros((48, N), f32)]
    for n in range(ITEMS):
        any_wants = mm(groups, jnp.where(wanted == n + 1, 1.0, 0.0)) > 0.5
        late = 0 if (n & 7) < cut else 1
        sums[late] += jnp.where(any_wants, 1.0, 0.0)
    early2, all2 = jnp.zeros((48, N), f32), jnp.zeros((48, N), f32)
    for t in range(3):
        s2, s3 = STRIDE[(t + 1) % 3], STRIDE[(t + 2) % 3]
        owners = jnp.where(lanes == digit(sub, s2) * 4 + digit(sub, s3), 1.0, 0.0)
        keep = (row48 >> 4 == t) & ((row48 & 3) != (lane48 >> 2)) & (lane48 < 16)
        early = mm(sums[0], owners)
        early2 = jnp.where(keep, early, early2)
        all2 = jnp.where(keep, early + mm(sums[1], owners), all2)
    chip = lax.broadcasted_iota(i32, (64, N), 0)
    lane64 = lax.broadcasted_iota(i32, (64, N), 1)
    pairs = jnp.where(lane64 >> 1 == chip, 1.0, 0.0)
    low = jnp.where((wanted > 0) & (((wanted - 1) & 7) < cut), 1.0, 0.0)
    every = jnp.where(wanted > 0, 1.0, 0.0)
    owners = jnp.zeros((N, N), f32)
    keep = lane64 < 12
    for t in range(3):
        s3 = STRIDE[(t + 2) % 3]
        owners = jnp.where(lanes == t * 4 + digit(sub, s3), 1.0, owners)
        keep = keep & (lane64 != t * 4 + digit(chip * 2, s3))
    early3 = jnp.where(keep, mm(mm(pairs, low), owners), 0.0)
    all3 = jnp.where(keep, mm(mm(pairs, every), owners), 0.0)
    out = jnp.zeros((8, N), f32)
    sub8 = lax.broadcasted_iota(i32, (8, N), 0)
    for n, x in enumerate((early2, all2, early3, all3)):
        top = jnp.max(jnp.max(x, axis=1, keepdims=True), axis=0, keepdims=True)
        out = jnp.where(sub8 == n, top, out)
    out_ref[...] = out.astype(i32)


def longest(cut, wanted):
    return pl.pallas_call(
        functools.partial(check_kernel, cut),
        out_shape=jax.ShapeDtypeStruct((8, N), jnp.int32),
        in_specs=[pl.BlockSpec(memory_space=pltpu.VMEM)],
        out_specs=pl.BlockSpec(memory_space=pltpu.VMEM),
        name="longest",
    )(wanted)


def make_plan(cut, caps2, caps3, place, wanted, requests):
    return pl.pallas_call(
        functools.partial(plan_kernel, cut, caps2, caps3),
        out_shape=jax.ShapeDtypeStruct((24, N), jnp.int32),
        grid_spec=pltpu.PrefetchScalarGridSpec(
            num_scalar_prefetch=1,
            grid=(1,),
            in_specs=[
                pl.BlockSpec((N, N), lambda i, t: (0, 0)),
                pl.BlockSpec((8, N), lambda i, t: (0, 0)),
            ],
            out_specs=pl.BlockSpec((24, N), lambda i, t: (0, 0)),
        ),
        name="plan",
    )(place, wanted, requests)


def pack_kernel(row, first, count, n_sources, table, *refs):
    sources, out, sem = refs[:n_sources], refs[n_sources], refs[n_sources + 1]

    def one(k, _):
        where = table[row, first + k]
        which = where // SHIFT
        pos = where - which * SHIFT
        pick(which, sources, lambda ref: pltpu.make_async_copy(ref.at[pos], out.at[k], sem).start())
        return 0

    lax.fori_loop(0, count, one, 0)
    pltpu.make_async_copy(out, out, sem).wait()


def pack(table, row, first, count, sources):
    rows = sources[0].shape[1]
    return pl.pallas_call(
        functools.partial(pack_kernel, row, first, count, len(sources)),
        out_shape=jax.ShapeDtypeStruct((count, rows, HD), jnp.bfloat16),
        in_specs=[pl.BlockSpec(memory_space=pltpu.SMEM)]
        + [pl.BlockSpec(memory_space=pl.ANY)] * len(sources),
        out_specs=pl.BlockSpec(memory_space=pltpu.VMEM),
        scratch_shapes=[pltpu.SemaphoreType.DMA],
        compiler_params=pltpu.CompilerParams(vmem_limit_bytes=12 * 1024 * 1024),
        name="pack",
    )(table, *sources)


def ring_pairs(axis):
    pairs = []
    for i in range(N):
        at = (i // STRIDE[axis]) % 4
        to = (at + (1 if i % 2 == 0 else 3)) % 4
        pairs.append((i, i + (to - at) * STRIDE[axis]))
    return pairs


def onward(x, axis):
    return lax.ppermute(x, "seq", ring_pairs(axis))


def swap(x):
    return lax.ppermute(x, "seq", [(i, i ^ 1) for i in range(N)])


def hop(pools, table, row, axis_of, cap):
    half = cap // 2
    first = [pack(table, t * 8 + row, cap, half, pools[t]) for t in range(3)]
    through = [onward(first[t], axis_of(t)) for t in range(3)]
    table, _ = lax.optimization_barrier((table, first))
    second = [pack(table, t * 8 + row, 0, cap, pools[t]) for t in range(3)]
    second, through = lax.optimization_barrier((second, through))
    direct = [onward(second[t], axis_of(t)) for t in range(3)]
    through, direct = lax.optimization_barrier((through, direct))
    passed = [onward(through[t], axis_of(t)) for t in range(3)]
    passed = lax.optimization_barrier(passed)
    return [[direct[t], swap(direct[t]), passed[t], swap(passed[t])] for t in range(3)]


def join(*lists):
    return [sum((x[t] for x in lists), []) for t in range(3)]


def route(cut, caps2, caps3, splits, queries, span_keys, span_values, past_keys, past_values, pools, place, wanted, requests, table):
    side = lambda t: (t + 1) % 3
    last = lambda t: (t + 2) % 3
    starts = (0, ROWS[0], ROWS[0] + ROWS[1])
    pieces = list(zip(starts, ROWS))
    two_a = hop(pools, table, 0, side, caps2[0])
    three_a = hop(join(pools, two_a), table, 2, last, caps3[0])
    groups = [join(pools, two_a, three_a)]
    if caps2[1]:
        two_b = hop(pools, table, 1, side, caps2[1])
        three_b = hop(join(pools, two_a, two_b), table, 3, last, caps3[1])
        groups.append(join(pools, two_a, two_b, three_a, three_b))
    out = None
    for ranges, found in zip(splits, groups):
        for first, many in ranges:
            out = attend(queries, span_keys, span_values, table, pieces, found, first, many, True, out)
    return out


FAST = (8, (44, 0), (48, 0), (((0, 8),),))


def dense(queries, span_keys, span_values, past_keys, past_values, pools, place, wanted, requests, table):
    me = lax.axis_index("seq")
    heads = span_keys.shape[1] // HD
    item = jnp.maximum(jnp.take(wanted, me, axis=1) - 1, 0)
    stacked = jnp.concatenate(
        [
            x.reshape(-1, BLOCK, heads, HD).transpose(0, 2, 1, 3).reshape(-1, BLOCK, HD)
            for x in (past_keys, past_values)
        ],
        axis=1,
    )
    arrived = lax.all_to_all(stacked[item], "seq", split_axis=0, concat_axis=0, tiled=True)
    slots = jnp.zeros((8, N), jnp.int32).at[4].set(requests[0])
    pieces = [(0, 2 * BLOCK)]
    return attend(queries, span_keys, span_values, slots, pieces, [[arrived]], 0, heads, False)


def shards(queries, span_keys, span_values, past_keys, past_values, selected):
    heads = selected.shape[1]
    me = lax.axis_index("seq")
    place = jnp.stack([me // 32, me // 8 % 4, me // 2 % 4, me % 2]).astype(jnp.int32)
    chosen = selected.reshape(-1)
    owners = chosen % N
    item = chosen // N * heads + lax.broadcasted_iota(jnp.int32, selected.shape, 1).reshape(-1)
    match = owners[None, :] == jnp.arange(N, dtype=jnp.int32)[:, None]
    outgoing = jnp.sum(jnp.where(match, item[None, :] + 1, 0), axis=1)
    copies = jnp.broadcast_to(outgoing, (N, 1, N))
    requests = jnp.pad(jnp.stack([owners, item]), ((0, 6), (0, N - owners.shape[0])))

    raw = [swap(past_keys), swap(past_values)]
    past_keys, past_values, copies = lax.optimization_barrier((past_keys, past_values, copies))
    wanted = lax.all_to_all(copies, "seq", split_axis=0, concat_axis=0, tiled=True).reshape(N, N)
    own = cut_items(past_keys, past_values)
    ahead = [onward(own[t], t) for t in range(3)]
    ahead, raw, wanted = lax.optimization_barrier((ahead, raw, wanted))
    twice = [onward(ahead[t], t) for t in range(3)]
    mate = cut_items(*raw)
    table = make_plan(*FAST[:3], place, wanted, requests)
    most = longest(FAST[0], wanted)[:4, 0]
    fits = jnp.all(most <= jnp.array([FAST[1][0], sum(FAST[1]), FAST[2][0], sum(FAST[2])]))
    twice, ahead, mate, table, fits = lax.optimization_barrier((twice, ahead, mate, table, fits))
    ahead_mate = [onward(mate[t], t) for t in range(3)]
    ahead_mate, twice = lax.optimization_barrier((ahead_mate, twice))
    pools = [
        [own[t], mate[t], ahead[t], ahead_mate[t], swap(ahead[t]), swap(ahead_mate[t]), twice[t], swap(twice[t])]
        for t in range(3)
    ]
    args = (queries, span_keys, span_values, past_keys, past_values, pools, place, wanted, requests, table)
    return lax.cond(fits, functools.partial(route, *FAST), dense, *args)


def solution(mesh):
    return jax.shard_map(
        shards,
        mesh=mesh,
        in_specs=(
            P("seq", None),
            P("seq", None),
            P("seq", None),
            P(None, "seq", None, None),
            P(None, "seq", None, None),
            P("seq", None, None),
        ),
        out_specs=P("seq", None),
        check_vma=False,
    )
```
